512 devices in a mesh: delay: 64 (over y, x, z_hi, core), row: 8 (over z_lo).
Axes of the slice: x: 4, y: 4, z: 16 (z_hi: 2, z_lo: 8; z = z_hi * 8 + z_lo), core: 2. Of those that a mesh axis runs over, the one named last changes fastest.
Arguments:
- excite: bfloat16 [1, 4096, 128], P(None, 'row'), may hold values from -6 to 6
- present_inverse: bfloat16 [32, 128, 128], P('row'), may hold values from -0.5 to 0.5
- retarded: bfloat16 [64, 32, 16, 128, 128], P('delay', 'row'), may hold values from -0.125 to 0.125
- columns: int32 [64, 32, 16], P('delay', 'row'), may hold values from 0 to 31, as said below
- future_in: float32 [64, 4096, 128], P('delay', 'row'), may hold values from -6 to 6
Outputs:
- currents: bfloat16 [1, 4096, 128], P(None, 'row')
- future_out: float32 [64, 4096, 128], P('delay', 'row')
The draws below stay inside these ranges and needn't reach their ends.
Inputs may be any that keep to these rules, and one draw needn't show every extreme that they name: `columns`: each block row at each delay names 16 different column blocks.
All inputs are finite; a program needn't handle non-finite values.
Results may differ from the reference program's by a relative error of at most 0.0052.
Values may be sent and summed in bfloat16 or wider, within the bound.
A program may use at most 64 MiB of HBM per device.

```python
import jax
import jax.numpy as jnp
from jax import lax

N_UNK = 4096
BLK = 128
NNZ = 16
EXC = 128
STEPS = 1
DELAYS = 64
BLOCKS = 32


def draw_columns(key, part):
    blocks = N_UNK // BLK
    subkeys = jax.random.split(jax.random.fold_in(key, 7), DELAYS * blocks)

    def pick_order(subkey):
        return jax.random.permutation(subkey, blocks)
    orders = jax.vmap(pick_order)(subkeys)
    return orders[:, :NNZ].reshape(DELAYS, blocks, NNZ).astype(jnp.int32)


def block_levels(key, extent, cuts, smallest, high):
    gain = 1.0
    for dim, shards_of in cuts:
        heights = jax.random.uniform(jax.random.fold_in(jax.random.fold_in(key, 6), dim), (shards_of,), jnp.float32, smallest / len(cuts), high / len(cuts))
        gain = gain * jnp.repeat(jnp.exp(heights), extent[dim] // shards_of).reshape((-1,) + (1,) * (len(extent) - 1 - dim))
    return gain


def bell_draw(own_key, extent, width, most, cuts=(), held_as=jnp.bfloat16):
    result = jax.random.normal(own_key, extent, jnp.float32) * width
    if len(cuts) > 0:
        result = block_levels(own_key, extent, cuts, -0.22, 0.18) * result
    return jnp.clip(result, min=-most, max=most).astype(held_as)


def setup_inputs(seed: int = 0) -> dict:
    keys = jax.random.split(jax.random.key(seed), 6)
    return {
        "excite": bell_draw(keys[0], (STEPS, N_UNK, EXC), 1.0, 6.0, ((1, 8),)),
        "present_inverse": bell_draw(keys[1], (BLOCKS, BLK, BLK), BLK ** -0.5, 0.5, ((0, 8),)),
        "retarded": bell_draw(keys[2], (DELAYS, BLOCKS, NNZ, BLK, BLK), (NNZ * BLK) ** -0.5, 0.125, ((0, 64), (1, 8))),
        "columns": draw_columns(jax.random.fold_in(keys[5], 71), 0),
        "future_in": bell_draw(keys[4], (DELAYS, N_UNK, EXC), 1.0, 6.0, ((0, 64), (1, 8)), jnp.float32),
    }


def reference(excite, present_inverse, retarded, columns, future_in):
    blocks = N_UNK // BLK
    future = future_in
    history = []
    for step in range(STEPS):
        right_side = (excite[step].astype(jnp.float32) - future[0]).astype(jnp.bfloat16)
        stacked = right_side.reshape(blocks, BLK, EXC).astype(jnp.float32)
        solved = jnp.einsum("rab,rbe->rae", present_inverse.astype(jnp.float32), stacked).astype(jnp.bfloat16)
        history.append(solved.reshape(N_UNK, EXC))
        shifted = jnp.concatenate([future[1:], jnp.zeros_like(future[:1])], 0)
        solved_wide = solved.astype(jnp.float32)

        def delay_term(pair):
            weights, indices = pair
            picked = solved_wide[indices.astype(jnp.int32)]
            return jnp.einsum("rkab,rkbe->rae", weights.astype(jnp.float32), picked).reshape(N_UNK, EXC)

        added = lax.map(delay_term, (retarded, columns))
        future = shifted + added
    return jnp.stack(history), future
```

```python
import functools

import jax
import jax.numpy as jnp
from jax import lax
from jax.experimental import pallas as pl
from jax.experimental.pallas import tpu as pltpu
from jax.sharding import PartitionSpec as P

MESH = pl.DeviceIdType.MESH
BLK = 128
ROWS = 512
RB = 4
NNZ = 16
WID = 128
LINE = 16
FAR = (8, 7, 9, 6, 10, 5, 11, 4, 12, 3, 13, 2, 14, 1, 15)
HOPS = (1, 3, 2)
ORDER = sorted(range(1, 32), key=lambda p: -(min((p // 4) % 4, 4 - (p // 4) % 4) + min(p % 4, 4 - p % 4)))


def gather_kernel(
    excite, inverse, future, whole, shift,
    ex_v, inv_v, fut_v, cast_v, sol_v, relay,
    load_sem, p1_send, p1_recv, rl_send, rl_recv, p2_send, p2_recv, p0_send,
    a_send, a_recv, b_send, b_recv, c_send, c_recv, sh_send, sh_recv,
):
    d = lax.axis_index("delay")
    r = lax.axis_index("row")
    core = d % 2
    zh = (d // 2) % 2
    x = (d // 4) % 4
    y = d // 16
    z = zh * 8 + r
    step_a = 4 + 12 * core
    step_b = 16 - 12 * core
    a = x * (1 - core) + y * core
    b = y * (1 - core) + x * core
    base = d - zh * 2
    mine = core * 16 + b * 4 + a
    near = zh == 0
    source = d == 0
    helper = d == 1

    def at_z(first, k):
        zz = k % LINE
        return (first + (zz // 8) * 2, zz % 8)

    def peer_a(k):
        return (d + ((a + k) % 4 - a) * step_a, r)

    def peer_b(k):
        return (d + ((b + k) % 4 - b) * step_b, r)

    partner = (d + 1 - 2 * core, r)

    barrier = pltpu.get_barrier_semaphore()

    def greet(device):
        pl.semaphore_signal(barrier, inc=1, device_id=device, device_id_type=MESH)

    @pl.when(near & (d != 0))
    def _():
        greet((0, r))

    on_root_line = base == 0
    line_sender = jnp.where(on_root_line, 1, base)
    for s in range(8):
        @pl.when((jnp.logical_not(near)) | (r != s))
        def _(s=s):
            greet((line_sender, s))
    @pl.when(helper)
    def _():
        greet((0, r))
    for k in HOPS:
        greet(peer_a(k))
        greet(peer_b(k))
    greet(partner)

    @pl.when(d < 63)
    def _():
        greet((d + 1, r))

    fut_in = pltpu.make_async_copy(future.at[0], fut_v, load_sem.at[0])
    fut_in.start()

    @pl.when(source)
    def _():
        ex_in = pltpu.make_async_copy(excite.at[0], ex_v, load_sem.at[1])
        inv_in = pltpu.make_async_copy(inverse, inv_v, load_sem.at[2])
        ex_in.start()
        inv_in.start()
        fut_in.wait()
        ex_in.wait()
        inv_in.wait()
        right = (ex_v[...].astype(jnp.float32) - fut_v[...]).astype(jnp.bfloat16)
        for k in range(RB):
            got = jnp.dot(inv_v[k], right[k * BLK:(k + 1) * BLK], preferred_element_type=jnp.float32)
            sol_v[pl.ds(k * 8, 8)] = got.astype(jnp.bfloat16).reshape(8, 16, WID)
        whole[0, r] = sol_v[0]
        pl.semaphore_wait(barrier, 31 + 7 + 1)
        for p in ORDER + [0]:
            pc, pb, pa = p // 16, (p // 4) % 4, p % 4
            px, py = (pa, pb) if pc == 0 else (pb, pa)
            if p == 0:
                continue
            pltpu.make_async_remote_copy(
                sol_v.at[p], whole.at[p, r], p1_send.at[p], p1_recv,
                device_id=((py * 4 + px) * 4 + pc, r), device_id_type=MESH,
            ).start()
        pltpu.make_async_remote_copy(
            sol_v.at[0], relay, rl_send, rl_recv, device_id=(1, r), device_id_type=MESH
        ).start()

    @pl.when(d > 0)
    def _():
        fut_in.wait()
        cast_v[...] = fut_v[...].astype(jnp.bfloat16)

    def shift_copy():
        return pltpu.make_async_remote_copy(
            cast_v, shift, sh_send, sh_recv, device_id=(d - 1, r), device_id_type=MESH
        )

    def line_copy(k):
        return pltpu.make_async_remote_copy(
            whole.at[mine, r], whole.at[mine, r], p2_send.at[k], p2_recv.at[r],
            device_id=at_z(base, z + k), device_id_type=MESH,
        )

    def root_copy(k):
        return pltpu.make_async_remote_copy(
            relay, whole.at[0, r], p0_send.at[k], p2_recv.at[r],
            device_id=at_z(0, z + k), device_id_type=MESH,
        )

    @pl.when(near & helper)
    def _():
        pl.semaphore_wait(barrier, 15 + 15 + 7 + 1)
        shift_copy().start()

    @pl.when(near & (d > 1))
    def _():
        pl.semaphore_wait(barrier, 15 + 7 + 1)

    @pl.when(jnp.logical_not(near))
    def _():
        pl.semaphore_wait(barrier, 7 + 1)
        shift_copy().start()

    @pl.when(near & (d > 1) & (core == 1))
    def _():
        shift_copy().start()

    @pl.when(near & (d > 0))
    def _():
        pltpu.make_async_remote_copy(
            sol_v.at[0], whole.at[mine, r], p1_send.at[0], p1_recv, device_id=(0, r), device_id_type=MESH
        ).wait_recv()
        for k in FAR:
            line_copy(k).start()

    @pl.when(helper)
    def _():
        pltpu.make_async_remote_copy(
            sol_v.at[0], relay, rl_send, rl_recv, device_id=(1, r), device_id_type=MESH
        ).wait_recv()
        for k in FAR:
            root_copy(k).start()

    @pl.when(near & (d > 1) & (core == 0))
    def _():
        shift_copy().start()

    for s in range(8):
        @pl.when((jnp.logical_not(near)) | (r != s))
        def _(s=s):
            pltpu.make_async_remote_copy(
                relay, whole.at[mine, s], p0_send.at[0], p2_recv.at[s], device_id=(0, r), device_id_type=MESH
            ).wait_recv()

    def slab(k, m):
        return core * 16 + ((b + 4 - m) % 4) * 4 + (a + 4 - k) % 4

    def other_slab(k, m):
        return (1 - core) * 16 + ((a + 4 - m) % 4) * 4 + (b + 4 - k) % 4

    def copy_a(k):
        return pltpu.make_async_remote_copy(
            whole.at[mine], whole.at[mine], a_send.at[k], a_recv.at[k],
            device_id=peer_a(k), device_id_type=MESH,
        )

    def copy_b(k, m):
        part = slab(k, 0)
        return pltpu.make_async_remote_copy(
            whole.at[part], whole.at[part], b_send.at[k, m], b_recv.at[k, m],
            device_id=peer_b(m), device_id_type=MESH,
        )

    def copy_c(k, m):
        part = slab(k, m)
        return pltpu.make_async_remote_copy(
            whole.at[part], whole.at[part], c_send.at[k, m], c_recv.at[k, m],
            device_id=partner, device_id_type=MESH,
        )

    def got(part, sem):
        pltpu.make_async_remote_copy(
            whole.at[part], whole.at[part], c_send.at[0, 0], sem, device_id=partner, device_id_type=MESH
        ).wait_recv()

    for k in HOPS:
        copy_a(k).start()
    for m in HOPS:
        copy_b(0, m).start()
    copy_c(0, 0).start()
    for k in HOPS:
        got(slab(k, 0), a_recv.at[k])
        for m in HOPS:
            copy_b(k, m).start()
        copy_c(k, 0).start()
    for k in (0,) + HOPS:
        for m in HOPS:
            got(slab(k, m), b_recv.at[k, m])
            copy_c(k, m).start()
    for k in (0,) + HOPS:
        for m in (0,) + HOPS:
            got(other_slab(k, m), c_recv.at[k, m])

    @pl.when(d < 63)
    def _():
        shift_copy().wait_recv()

    @pl.when(d == 63)
    def _():
        shift[...] = jnp.zeros_like(shift)

    @pl.when(source)
    def _():
        for p in ORDER:
            pltpu.make_async_remote_copy(
                sol_v.at[p], whole.at[p, r], p1_send.at[p], p1_recv, device_id=partner, device_id_type=MESH
            ).wait_send()
        pltpu.make_async_remote_copy(
            sol_v.at[0], relay, rl_send, rl_recv, device_id=partner, device_id_type=MESH
        ).wait_send()

    @pl.when(d > 0)
    def _():
        shift_copy().wait_send()

    @pl.when(near & (d > 0))
    def _():
        for k in FAR:
            line_copy(k).wait_send()

    @pl.when(helper)
    def _():
        for k in FAR:
            root_copy(k).wait_send()

    for k in HOPS:
        copy_a(k).wait_send()
    for k in (0,) + HOPS:
        for m in HOPS:
            copy_b(k, m).wait_send()
    for k in (0,) + HOPS:
        for m in (0,) + HOPS:
            copy_c(k, m).wait_send()


def apply_kernel(row, columns, whole, weights, shift, currents, out):
    r = row[0]
    currents[0] = whole[:, r].reshape(ROWS, WID)
    for i in range(RB):
        left = jnp.concatenate([weights[0, i, k] for k in range(NNZ)], axis=1)
        picked = []
        for k in range(NNZ):
            j = columns[0, i, k]
            quarter = whole[pl.ds((j % 4) * 8, 8), j // 4]
            picked.append(quarter.reshape(BLK, WID))
        right = jnp.concatenate(picked, axis=0)
        total = jnp.dot(left, right, preferred_element_type=jnp.float32)
        rows = pl.ds(i * BLK, BLK)
        out[0, rows] = total + shift[rows].astype(jnp.float32)


def per_device(excite, present_inverse, retarded, columns, future_in):
    vmem = pl.BlockSpec(memory_space=pltpu.VMEM)
    smem = pl.BlockSpec(memory_space=pltpu.SMEM)
    hbm = pl.BlockSpec(memory_space=pl.ANY)
    dma = pltpu.SemaphoreType.DMA
    whole, shift = pl.pallas_call(
        gather_kernel,
        out_shape=(
            jax.ShapeDtypeStruct((32, 8, 16, WID), jnp.bfloat16),
            jax.ShapeDtypeStruct((ROWS, WID), jnp.bfloat16),
        ),
        in_specs=[hbm, hbm, hbm],
        out_specs=(vmem, vmem),
        scratch_shapes=[
            pltpu.VMEM((ROWS, WID), jnp.bfloat16),
            pltpu.VMEM((RB, BLK, BLK), jnp.bfloat16),
            pltpu.VMEM((ROWS, WID), jnp.float32),
            pltpu.VMEM((ROWS, WID), jnp.bfloat16),
            pltpu.VMEM((32, 16, WID), jnp.bfloat16),
            pltpu.VMEM((16, WID), jnp.bfloat16),
            dma((3,)), dma((32,)), dma, dma, dma, dma((16,)), dma((8,)), dma((16,)),
            dma((4,)), dma((4,)), dma((4, 4)), dma((4, 4)), dma((4, 4)), dma((4, 4)), dma, dma,
        ],
        compiler_params=pltpu.CompilerParams(collective_id=0, has_side_effects=True),
        name="gather",
    )(excite, present_inverse, future_in)
    row = lax.axis_index("row").astype(jnp.int32).reshape(1)
    return pl.pallas_call(
        apply_kernel,
        out_shape=(
            jax.ShapeDtypeStruct((1, ROWS, WID), jnp.bfloat16),
            jax.ShapeDtypeStruct((1, ROWS, WID), jnp.float32),
        ),
        in_specs=[smem, smem, vmem, vmem, vmem],
        out_specs=(vmem, vmem),
        name="apply",
    )(row, columns, whole, retarded, shift)


def solution(mesh):
    return jax.shard_map(
        per_device,
        mesh=mesh,
        in_specs=(
            P(None, "row", None),
            P("row", None, None),
            P("delay", "row", None, None, None),
            P("delay", "row", None),
            P("delay", "row", None),
        ),
        out_specs=(P(None, "row", None), P("delay", "row", None)),
        check_vma=False,
    )
```

```python
import jax
import jax.numpy as jnp
from jax import lax
from jax.experimental import pallas as pl
from jax.experimental.pallas import tpu as pltpu
from jax.sharding import PartitionSpec as P

MESH = pl.DeviceIdType.MESH
BLK = 128
ROWS = 512
RB = 4
NNZ = 16
WID = 128
HOPS = (1, 3, 2)
REACH = 4


def step_kernel(
    excite, inverse, weights, columns, future, currents, out,
    ex_v, inv_v, w_v, col_s, fut_v, cast_v, shift_v, half_v, src_v, row_v, whole,
    load_sem, half_send, half_recv, one_send, one_recv, few_send, few_recv,
    line_send, line_recv, fwd_send, ready, ready_shift,
    a_send, a_recv, b_send, b_recv, c_send, c_recv, sh_send, sh_recv,
):
    d = lax.axis_index("delay")
    r = lax.axis_index("row")
    core = d % 2
    zh = (d // 2) % 2
    x = (d // 4) % 4
    y = d // 16
    z = zh * 8 + r
    step_a = 4 + 12 * core
    step_b = 16 - 12 * core
    a = x * (1 - core) + y * core
    b = y * (1 - core) + x * core
    base = d - zh * 2
    mine = core * 16 + b * 4 + a
    near = zh == 0
    far = zh == 1
    root = (x + y + zh) == 0
    source = d == 0
    partner = (d + 1 - 2 * core, r)

    def rank_of(line):
        return jnp.where(line < 8, line, 23 - line)

    rank = rank_of(z)

    def wrapped(k):
        return (z + k + 16) % 16

    def at_z(k):
        n = wrapped(k)
        return (base + (n // 8) * 2, n % 8)

    def later(k):
        return rank_of(wrapped(k)) > rank

    def peer_a(k):
        return (d + ((a + k) % 4 - a) * step_a, r)

    def peer_b(k):
        return (d + ((b + k) % 4 - b) * step_b, r)

    def remote(src, dst, send, recv, device):
        return pltpu.make_async_remote_copy(src, dst, send, recv, device_id=device, device_id_type=MESH)

    barrier = pltpu.get_barrier_semaphore()

    def greet(device):
        pl.semaphore_signal(barrier, inc=1, device_id=device, device_id_type=MESH)

    fut_in = pltpu.make_async_copy(future.at[0], fut_v, load_sem.at[0])
    fut_in.start()

    for k in HOPS:
        greet(peer_a(k))
        greet(peer_b(k))
    greet(partner)
    greeted = 7
    steps = [s * k for k in range(1, REACH + 1) for s in (1, -1)]
    for k in steps:
        @pl.when(later(k))
        def _(k=k):
            greet(at_z(k))
        greeted = greeted + jnp.where(later(k), 0, 1)

    @pl.when((d % 4 == 1))
    def _():
        greet((d + 1, r))

    @pl.when((d % 4 == 0) & (d > 0))
    def _():
        greet((d - 1, r))

    greeted = greeted + jnp.where(d % 4 == 2, 1, 0) + jnp.where((d % 4 == 3) & (d < 63), 1, 0)

    w_in = pltpu.make_async_copy(weights.at[0], w_v, load_sem.at[3])
    col_in = pltpu.make_async_copy(columns.at[0], col_s, load_sem.at[4])
    ex_in = pltpu.make_async_copy(excite.at[0], ex_v, load_sem.at[1])
    inv_in = pltpu.make_async_copy(inverse, inv_v, load_sem.at[2])

    @pl.when(source)
    def _():
        ex_in.start()
        inv_in.start()
        fut_in.wait()
        ex_in.wait()
        inv_in.wait()
        right = (ex_v[...].astype(jnp.float32) - fut_v[...]).astype(jnp.bfloat16)
        for k in range(RB):
            got = jnp.dot(inv_v[k], right[k * BLK:(k + 1) * BLK], preferred_element_type=jnp.float32)
            cut = got.astype(jnp.bfloat16).reshape(8, 16, WID)
            if k < 2:
                src_v[pl.ds(k * 8, 8)] = cut
            else:
                half_v[pl.ds(k * 8 - 16, 8)] = cut
            if k == 0:
                whole[0, r] = cut[0]

    w_in.start()
    col_in.start()

    @pl.when(d > 0)
    def _():
        fut_in.wait()
        cast_v[...] = fut_v[...].astype(jnp.bfloat16)

    pl.semaphore_wait(barrier, greeted)

    for k in steps:
        n = wrapped(k)
        sends = (n < 8) | ((n >= 12) & far & (n - z <= 3))
        @pl.when(jnp.logical_not(later(k)) & sends)
        def _(k=k):
            pl.semaphore_signal(ready.at[REACH - k], inc=1, device_id=at_z(k), device_id_type=MESH)

    @pl.when((d % 4 == 3) & (d < 63))
    def _():
        pl.semaphore_signal(ready_shift, inc=1, device_id=(d + 1, r), device_id_type=MESH)

    half_one = remote(half_v.at[0], whole.at[16, r], half_send.at[0], one_recv, partner)
    half_rest = remote(half_v.at[pl.ds(1, 15)], src_v.at[pl.ds(1, 15)], half_send.at[1], half_recv, partner)

    @pl.when(source)
    def _():
        half_rest.start()
        half_one.start()

    def root_one(k):
        return remote(src_v.at[k * 4], whole.at[core * 16 + k * 4, r], one_send.at[k], one_recv, peer_b(k))

    def root_few(k):
        return remote(
            src_v.at[pl.ds(k * 4 + 1, 3)], row_v.at[pl.ds(1, 3)], few_send.at[k], few_recv, peer_b(k)
        )

    def root_own(k):
        return remote(src_v.at[k], whole.at[core * 16 + k, r], one_send.at[3 + k], one_recv, peer_a(k))

    def row_one(k):
        return remote(row_v.at[k], whole.at[core * 16 + b * 4 + k, r], one_send.at[k], one_recv, peer_a(k))

    @pl.when(root & (core == 1))
    def _():
        half_rest.wait_recv()

    @pl.when(root)
    def _():
        for k in (2, 1, 3):
            root_few(k).start()
        for k in (2, 1, 3):
            root_one(k).start()
            root_own(k).start()

    head = near & (a == 0) & (b > 0)

    @pl.when(head)
    def _():
        root_few(1).wait_recv()
        for k in (2, 1, 3):
            row_one(k).start()

    shift_copy = remote(cast_v, shift_v, sh_send, sh_recv, (d - 1, r))

    @pl.when(core == 1)
    def _():
        shift_copy.start()

    @pl.when(near & (d > 0))
    def _():
        root_own(1).wait_recv()

    def line_copy(k):
        return remote(whole.at[mine, r], whole.at[mine, r], line_send.at[REACH + k], line_recv.at[r], at_z(k))

    @pl.when(near)
    def _():
        for k in (4, 3, 2, 1):
            @pl.when(jnp.logical_not(later(-k)))
            def _(k=k):
                line_copy(-k).start()
        for k in (1, 2, 3, 4):
            pl.semaphore_wait(ready.at[REACH + k], 1)
            line_copy(k).start()
        for k in (1, 2, 3, 4):
            @pl.when(later(-k))
            def _(k=k):
                pl.semaphore_wait(ready.at[REACH - k], 1)
                line_copy(-k).start()

    def fwd_copy(k):
        s = z - 4 if k > 0 else (z + 4) % 16
        return remote(
            whole.at[mine, s], whole.at[mine, s], fwd_send.at[REACH + k], line_recv.at[s], at_z(k)
        )

    def got_piece(s):
        remote(whole.at[mine, s], whole.at[mine, s], half_send.at[0], line_recv.at[s], partner).wait_recv()

    def slab(k, m):
        return core * 16 + ((b + 4 - m) % 4) * 4 + (a + 4 - k) % 4

    def other_slab(k, m):
        return (1 - core) * 16 + ((a + 4 - m) % 4) * 4 + (b + 4 - k) % 4

    def part(p, g):
        return whole.at[p]

    def copy_a(g, k):
        here = part(mine, g)
        return remote(here, here, a_send.at[g, k], a_recv.at[g, k], peer_a(k))

    def copy_b(g, k, m):
        here = part(slab(k, 0), g)
        return remote(here, here, b_send.at[g, k, m], b_recv.at[g, k, m], peer_b(m))

    def copy_c(g, k, m):
        here = part(slab(k, m), g)
        return remote(here, here, c_send.at[g, k, m], c_recv.at[g, k, m], partner)

    def got(g, p, sem):
        here = part(p, g)
        remote(here, here, half_send.at[0], sem, partner).wait_recv()

    plus = [((z >= 4) & (z < 8)), ((z >= 8) & (z < 12))]
    minus = [(z >= 12), (z < 4)]
    for h in range(2):
        @pl.when(plus[h])
        def _():
            got_piece(z - 4)
            for k in (1, 2, 3, 4):
                fwd_copy(k).start()

        @pl.when(minus[h])
        def _(h=h):
            got_piece((z + 4) % 16)
            for k in (-1, -2, -3):
                if h == 0:
                    pl.semaphore_wait(ready.at[REACH + k], 1)
                fwd_copy(k).start()

    for g in range(1):
        for s in range(8):
            passed = ((z < 12) & (z - 4 == s)) | (((z >= 12) | (z < 4)) & ((z + 4) % 16 == s))

            @pl.when((far | (r != s)) & jnp.logical_not(passed))
            def _(s=s):
                got_piece(s)

        for k in HOPS:
            copy_a(g, k).start()
        for m in HOPS:
            copy_b(g, 0, m).start()
        copy_c(g, 0, 0).start()

        @pl.when((core == 0) & far)
        def _():
            shift_copy.start()

        @pl.when((core == 0) & near & (d > 0))
        def _():
            pl.semaphore_wait(ready_shift, 1)
            shift_copy.start()

        for k in HOPS:
            got(g, slab(k, 0), a_recv.at[g, k])
            for m in HOPS:
                copy_b(g, k, m).start()
            copy_c(g, k, 0).start()
        for k in (0,) + HOPS:
            for m in HOPS:
                got(g, slab(k, m), b_recv.at[g, k, m])
                copy_c(g, k, m).start()

    w_in.wait()
    col_in.wait()
    for g in range(1):
        for k in (0,) + HOPS:
            for m in (0,) + HOPS:
                got(g, other_slab(k, m), c_recv.at[g, k, m])

    @pl.when(d < 63)
    def _():
        shift_copy.wait_recv()

    @pl.when(d == 63)
    def _():
        shift_v[...] = jnp.zeros_like(shift_v)

    currents[0] = whole[:, r].reshape(ROWS, WID)
    for i in range(RB):
        left = jnp.concatenate([w_v[i, k] for k in range(NNZ)], axis=1)
        picked = []
        for k in range(NNZ):
            j = col_s[i, k]
            picked.append(whole[pl.ds((j % 4) * 8, 8), j // 4].reshape(BLK, WID))
        total = jnp.dot(left, jnp.concatenate(picked, axis=0), preferred_element_type=jnp.float32)
        rows = pl.ds(i * BLK, BLK)
        out[0, rows] = total + shift_v[rows].astype(jnp.float32)

    @pl.when(source)
    def _():
        half_rest.wait_send()
        half_one.wait_send()

    @pl.when(root)
    def _():
        for k in (1, 2, 3):
            root_few(k).wait_send()
            root_one(k).wait_send()
            root_own(k).wait_send()

    @pl.when(head)
    def _():
        for k in (1, 2, 3):
            row_one(k).wait_send()

    @pl.when(d > 0)
    def _():
        shift_copy.wait_send()

    @pl.when(near)
    def _():
        for k in steps:
            line_copy(k).wait_send()

    @pl.when(plus[0] | plus[1])
    def _():
        for k in (1, 2, 3, 4):
            fwd_copy(k).wait_send()

    @pl.when(minus[0] | minus[1])
    def _():
        for k in (-1, -2, -3):
            fwd_copy(k).wait_send()

    for g in range(1):
        for k in HOPS:
            copy_a(g, k).wait_send()
        for k in (0,) + HOPS:
            for m in HOPS:
                copy_b(g, k, m).wait_send()
        for k in (0,) + HOPS:
            for m in (0,) + HOPS:
                copy_c(g, k, m).wait_send()


def write_kernel(currents, out, currents_out, out_out, sem):
    first = pltpu.make_async_copy(out, out_out, sem.at[0])
    second = pltpu.make_async_copy(currents, currents_out, sem.at[1])
    first.start()
    second.start()
    first.wait()
    second.wait()


def per_device(excite, present_inverse, retarded, columns, future_in):
    hbm = pl.BlockSpec(memory_space=pltpu.HBM)
    vmem = pl.BlockSpec(memory_space=pltpu.VMEM)
    dma = pltpu.SemaphoreType.DMA
    flag = pltpu.SemaphoreType.REGULAR
    half, single = jnp.bfloat16, jnp.float32
    results = (
        jax.ShapeDtypeStruct((1, ROWS, WID), half),
        jax.ShapeDtypeStruct((1, ROWS, WID), single),
    )
    held = pl.pallas_call(
        step_kernel,
        out_shape=(pltpu.VMEM((1, ROWS, WID), half), pltpu.VMEM((1, ROWS, WID), single)),
        in_specs=[hbm] * 5,
        out_specs=(vmem, vmem),
        scratch_shapes=[
            pltpu.VMEM((ROWS, WID), half),
            pltpu.VMEM((RB, BLK, BLK), half),
            pltpu.VMEM((RB, NNZ, BLK, BLK), half),
            pltpu.SMEM((RB, NNZ), jnp.int32),
            pltpu.VMEM((ROWS, WID), single),
            pltpu.VMEM((ROWS, WID), half),
            pltpu.VMEM((ROWS, WID), half),
            pltpu.VMEM((16, 16, WID), half),
            pltpu.VMEM((16, 16, WID), half),
            pltpu.VMEM((4, 16, WID), half),
            pltpu.VMEM((32, 8, 16, WID), half),
            dma((5,)), dma((2,)), dma, dma((8,)), dma, dma((4,)), dma,
            dma((9,)), dma((8,)), dma((9,)), flag((9,)), flag,
            dma((1, 4)), dma((1, 4)), dma((1, 4, 4)), dma((1, 4, 4)), dma((1, 4, 4)), dma((1, 4, 4)), dma, dma,
        ],
        compiler_params=pltpu.CompilerParams(collective_id=0, has_side_effects=True, vmem_limit_bytes=56 << 20),
        name="step",
    )(excite, present_inverse, retarded, columns, future_in)
    return pl.pallas_call(
        write_kernel,
        out_shape=results,
        in_specs=[vmem, vmem],
        out_specs=(hbm, hbm),
        scratch_shapes=[dma((2,))],
        compiler_params=pltpu.CompilerParams(vmem_limit_bytes=4 << 20),
        name="write",
    )(*held)


def solution(mesh):
    return jax.shard_map(
        per_device,
        mesh=mesh,
        in_specs=(
            P(None, "row", None),
            P("row", None, None),
            P("delay", "row", None, None, None),
            P("delay", "row", None),
            P("delay", "row", None),
        ),
        out_specs=(P(None, "row", None), P("delay", "row", None)),
        check_vma=False,
    )
```

```python
import jax
import jax.numpy as jnp
from jax import lax
from jax.experimental import pallas as pl
from jax.experimental.pallas import tpu as pltpu
from jax.sharding import PartitionSpec as P

MESH = pl.DeviceIdType.MESH
BLK = 128
ROWS = 512
RB = 4
NNZ = 16
WID = 128
HOPS = (1, 3, 2)
SENDS = (2, 1, 3)
REACH = 4


def step_kernel(
    excite, inverse, weights, columns, future, currents, out,
    ex_v, inv_v, w_v, col_s, fut_v, cast_v, shift_v, pass_v, half_v, src_v, row_v, whole,
    load_sem, pass_send, pass_recv, half_send, half_recv, one_send, one_recv, few_send, few_recv,
    line_send, line_recv, fwd_send, ready, ready_shift,
    all_send, a_recv, b_recv, c_recv, sh_send, sh_recv,
):
    d = lax.axis_index("delay")
    r = lax.axis_index("row")
    core = d % 2
    zh = (d // 2) % 2
    x = (d // 4) % 4
    y = d // 16
    z = zh * 8 + r
    step_a = 4 + 12 * core
    step_b = 16 - 12 * core
    a = x * (1 - core) + y * core
    b = y * (1 - core) + x * core
    base = d - zh * 2
    mine = core * 16 + b * 4 + a
    near = zh == 0
    far = zh == 1
    root = (x + y + zh) == 0
    source = d == 0
    partner = (d + 1 - 2 * core, r)

    def rank_of(line):
        return jnp.where(line < 8, line, 23 - line)

    rank = rank_of(z)

    def wrapped(k):
        return (z + k + 16) % 16

    def at_z(k):
        n = wrapped(k)
        return (base + (n // 8) * 2, n % 8)

    def later(k):
        return rank_of(wrapped(k)) > rank

    def peer_a(k):
        return (d + ((a + k) % 4 - a) * step_a, r)

    def peer_b(k):
        return (d + ((b + k) % 4 - b) * step_b, r)

    def remote(src, dst, send, recv, device):
        return pltpu.make_async_remote_copy(src, dst, send, recv, device_id=device, device_id_type=MESH)

    barrier = pltpu.get_barrier_semaphore()

    def greet(device):
        pl.semaphore_signal(barrier, inc=1, device_id=device, device_id_type=MESH)

    fut_in = pltpu.make_async_copy(future.at[0], fut_v, load_sem.at[0])
    fut_in.start()

    for k in HOPS:
        greet(peer_a(k))
        greet(peer_b(k))
    greet(partner)
    greeted = 7
    steps = [s * k for k in range(1, REACH + 1) for s in (1, -1)]
    for k in steps:
        @pl.when(later(k))
        def _(k=k):
            greet(at_z(k))
        greeted = greeted + jnp.where(later(k), 0, 1)
    for k in (5, 6, 7):
        @pl.when(z + k < 8)
        def _(k=k):
            greet(at_z(k))
        greeted = greeted + jnp.where(near & (z >= k), 1, 0)

    @pl.when((d % 4 == 1))
    def _():
        greet((d + 2, r))

    @pl.when((d % 4 == 0) & (d > 0))
    def _():
        greet((d - 1, r))

    greeted = greeted + jnp.where(d % 4 == 3, 1, 0) + jnp.where((d % 4 == 3) & (d < 63), 1, 0)

    w_in = pltpu.make_async_copy(weights.at[0], w_v, load_sem.at[3])
    col_in = pltpu.make_async_copy(columns.at[0], col_s, load_sem.at[4])
    ex_in = pltpu.make_async_copy(excite.at[0], ex_v, load_sem.at[1])
    inv_in = pltpu.make_async_copy(inverse, inv_v, load_sem.at[2])

    @pl.when(source)
    def _():
        ex_in.start()
        inv_in.start()
        fut_in.wait()
        ex_in.wait()
        inv_in.wait()
        right = (ex_v[...].astype(jnp.float32) - fut_v[...]).astype(jnp.bfloat16)
        for k in range(RB):
            got = jnp.dot(inv_v[k], right[k * BLK:(k + 1) * BLK], preferred_element_type=jnp.float32)
            cut = got.astype(jnp.bfloat16).reshape(8, 16, WID)
            if k < 2:
                src_v[pl.ds(k * 8, 8)] = cut
            else:
                half_v[pl.ds(k * 8 - 16, 8)] = cut
            if k == 0:
                whole[0, r] = cut[0]

    w_in.start()
    col_in.start()

    @pl.when(d > 0)
    def _():
        fut_in.wait()
        cast_v[...] = fut_v[...].astype(jnp.bfloat16)

    pl.semaphore_wait(barrier, greeted)

    for k in steps:
        n = wrapped(k)
        sends = (n < 8) | ((n >= 12) & far & (n - z <= 3))
        @pl.when(jnp.logical_not(later(k)) & sends)
        def _(k=k):
            pl.semaphore_signal(ready.at[REACH - k], inc=1, device_id=at_z(k), device_id_type=MESH)

    @pl.when((d % 4 == 3) & (d < 63))
    def _():
        pl.semaphore_signal(ready_shift, inc=1, device_id=(d + 1, r), device_id_type=MESH)

    half_one = remote(half_v.at[0], whole.at[16, r], half_send, one_recv, partner)
    half_rest = remote(half_v.at[pl.ds(1, 15)], src_v.at[pl.ds(1, 15)], half_send, half_recv, partner)

    @pl.when(source)
    def _():
        half_rest.start()
        half_one.start()

    def root_one(k):
        return remote(src_v.at[k * 4], whole.at[core * 16 + k * 4, r], one_send, one_recv, peer_b(k))

    def root_few(k):
        return remote(
            src_v.at[pl.ds(k * 4 + 1, 3)], row_v.at[pl.ds(1, 3)], few_send, few_recv, peer_b(k)
        )

    def root_own(k):
        return remote(src_v.at[k], whole.at[core * 16 + k, r], one_send, one_recv, peer_a(k))

    def row_one(k):
        return remote(row_v.at[k], whole.at[core * 16 + b * 4 + k, r], one_send, one_recv, peer_a(k))

    @pl.when(root & (core == 1))
    def _():
        half_rest.wait_recv()

    @pl.when(root)
    def _():
        for k in (2, 1, 3):
            root_few(k).start()
        for k in (2, 1, 3):
            root_one(k).start()
            root_own(k).start()

    head = near & (a == 0) & (b > 0)

    @pl.when(head)
    def _():
        root_few(1).wait_recv()
        for k in (2, 1, 3):
            row_one(k).start()

    shift_copy = remote(cast_v, shift_v, sh_send, sh_recv, (d - 1, r))

    handed = remote(cast_v, pass_v, pass_send, pass_recv, partner)
    passed_on = remote(pass_v, shift_v, pass_send, sh_recv, (d - 2, r))

    @pl.when(core == 1)
    def _():
        shift_copy.start()

    @pl.when(far & (core == 0))
    def _():
        handed.start()

    @pl.when(near & (d > 0))
    def _():
        root_own(1).wait_recv()

    def line_copy(k):
        return remote(whole.at[mine, r], whole.at[mine, r], line_send, line_recv.at[r], at_z(k))

    @pl.when(near)
    def _():
        for k in (7, 6, 5, 4, 3, 2, 1):
            @pl.when(z >= k)
            def _(k=k):
                line_copy(-k).start()
        for k in (1, 2, 3, 4):
            pl.semaphore_wait(ready.at[REACH + k], 1)
            line_copy(k).start()
        for k in (1, 2, 3, 4):
            @pl.when(later(-k))
            def _(k=k):
                pl.semaphore_wait(ready.at[REACH - k], 1)
                line_copy(-k).start()

    def fwd_copy(k):
        s = z - 4 if k > 0 else (z + 4) % 16
        return remote(
            whole.at[mine, s], whole.at[mine, s], fwd_send, line_recv.at[s], at_z(k)
        )

    def got_piece(s):
        remote(whole.at[mine, s], whole.at[mine, s], half_send, line_recv.at[s], partner).wait_recv()

    def slab(k):
        return core * 16 + b * 4 + (a + 4 - k) % 4

    def part(p, g):
        return whole.at[p, pl.ds(g * 4, 4)]

    def lane(m, g):
        return whole.at[pl.ds(core * 16 + ((b + 4 - m) % 4) * 4, 4), pl.ds(g * 4, 4)]

    def copy_a(g, k):
        here = part(mine, g)
        return remote(here, here, all_send, a_recv.at[g, k - 1], peer_a(k))

    def copy_b(g, k, m):
        here = part(slab(k), g)
        return remote(here, here, all_send, b_recv.at[g, m - 1], peer_b(m))

    def copy_c(g, m):
        here = lane(m, g)
        return remote(here, here, all_send, c_recv, partner)

    plus = [((z >= 4) & (z < 8)), ((z >= 8) & (z < 12))]
    minus = [(z >= 12), (z < 4)]
    def forward_up(h):
        @pl.when(plus[h])
        def _():
            got_piece(z - 4)
            for k in (4, 3, 2, 1):
                fwd_copy(k).start()

    def forward_down(h):
        @pl.when(minus[h])
        def _():
            got_piece((z + 4) % 16)
            for k in (-3, -2, -1):
                if h == 0:
                    pl.semaphore_wait(ready.at[REACH + k], 1)
                    fwd_copy(k).start()
                else:
                    @pl.when(z + k < 0)
                    def _(k=k):
                        fwd_copy(k).start()

    def pieces(g):
        for s in range(g * 4, g * 4 + 4):
            passed = (plus[g] & (z - 4 == s)) | (minus[g] & ((z + 4) % 16 == s))

            @pl.when((far | (r != s)) & jnp.logical_not(passed))
            def _(s=s):
                got_piece(s)

    def spread(g):
        for k in SENDS:
            copy_a(g, k).start()
        for m in SENDS:
            copy_b(g, 0, m).start()

    def pass_on(g):
        for k in HOPS:
            copy_a(g, k).wait_recv()
            for m in SENDS:
                copy_b(g, k, m).start()
        copy_c(g, 0).start()

    def share(g):
        for m in HOPS:
            here = lane(m, g)
            remote(here, here, all_send, b_recv.at[g, m - 1], partner).wait_recv()
            copy_c(g, m).start()

    forward_up(0)
    forward_down(0)
    forward_up(1)

    @pl.when(far & (core == 1))
    def _():
        handed.wait_recv()
        passed_on.start()

    pieces(0)
    spread(0)
    forward_down(1)
    pass_on(0)
    pieces(1)
    spread(1)

    share(0)
    pass_on(1)

    @pl.when((core == 0) & near & (d > 0))
    def _():
        pl.semaphore_wait(ready_shift, 1)
        shift_copy.start()

    share(1)

    def drained(src, sem):
        remote(src, src, sem, c_recv, partner).wait_send()

    @pl.when(source)
    def _():
        drained(src_v, half_send)

    @pl.when(root)
    def _():
        drained(src_v.at[pl.ds(0, 9)], few_send)
        drained(src_v.at[pl.ds(0, 6)], one_send)

    @pl.when(head)
    def _():
        drained(src_v.at[pl.ds(0, 3)], one_send)

    for low, high, count in ((0, 4, 8), (5, 5, 9), (6, 6, 10), (7, 7, 11)):
        @pl.when((z >= low) & (z <= high))
        def _(count=count):
            drained(src_v.at[pl.ds(0, count)], line_send)

    for low, high, count in ((0, 0, 3), (1, 1, 2), (2, 2, 1), (4, 11, 4), (12, 15, 3)):
        @pl.when((z >= low) & (z <= high))
        def _(count=count):
            drained(src_v.at[pl.ds(0, count)], fwd_send)

    w_in.wait()
    col_in.wait()
    there = whole.at[pl.ds(0, 16)]
    remote(there, there, all_send, c_recv, partner).wait_recv()

    @pl.when(d < 63)
    def _():
        shift_copy.wait_recv()

    @pl.when(d == 63)
    def _():
        shift_v[...] = jnp.zeros_like(shift_v)

    currents[0] = whole[:, r].reshape(ROWS, WID)
    for i in range(RB):
        left = jnp.concatenate([w_v[i, k] for k in range(NNZ)], axis=1)
        picked = []
        for k in range(NNZ):
            j = col_s[i, k]
            picked.append(whole[pl.ds((j % 4) * 8, 8), j // 4].reshape(BLK, WID))
        total = jnp.dot(left, jnp.concatenate(picked, axis=0), preferred_element_type=jnp.float32)
        rows = pl.ds(i * BLK, BLK)
        out[0, rows] = total + shift_v[rows].astype(jnp.float32)

    drained(whole.at[pl.ds(0, 31)], all_send)

    @pl.when((d > 0) & (near | (core == 1)))
    def _():
        shift_copy.wait_send()

    @pl.when(far & (core == 0))
    def _():
        handed.wait_send()

    @pl.when(far & (core == 1))
    def _():
        passed_on.wait_send()


def write_kernel(currents, out, currents_out, out_out, sem):
    first = pltpu.make_async_copy(out, out_out, sem.at[0])
    second = pltpu.make_async_copy(currents, currents_out, sem.at[1])
    first.start()
    second.start()
    first.wait()
    second.wait()


def per_device(excite, present_inverse, retarded, columns, future_in):
    hbm = pl.BlockSpec(memory_space=pl.ANY)
    vmem = pl.BlockSpec(memory_space=pltpu.VMEM)
    dma = pltpu.SemaphoreType.DMA
    flag = pltpu.SemaphoreType.REGULAR
    half, single = jnp.bfloat16, jnp.float32
    results = (
        jax.ShapeDtypeStruct((1, ROWS, WID), half),
        jax.ShapeDtypeStruct((1, ROWS, WID), single),
    )
    held = pl.pallas_call(
        step_kernel,
        out_shape=(pltpu.VMEM((1, ROWS, WID), half), pltpu.VMEM((1, ROWS, WID), single)),
        in_specs=[hbm] * 5,
        out_specs=(vmem, vmem),
        scratch_shapes=[
            pltpu.VMEM((ROWS, WID), half),
            pltpu.VMEM((RB, BLK, BLK), half),
            pltpu.VMEM((RB, NNZ, BLK, BLK), half),
            pltpu.SMEM((RB, NNZ), jnp.int32),
            pltpu.VMEM((ROWS, WID), single),
            pltpu.VMEM((ROWS, WID), half),
            pltpu.VMEM((ROWS, WID), half),
            pltpu.VMEM((ROWS, WID), half),
            pltpu.VMEM((16, 16, WID), half),
            pltpu.VMEM((16, 16, WID), half),
            pltpu.VMEM((4, 16, WID), half),
            pltpu.VMEM((32, 8, 16, WID), half),
            dma((5,)), dma, dma, dma, dma, dma, dma, dma, dma,
            dma, dma((8,)), dma, flag((9,)), flag,
            dma, dma((2, 3)), dma((2, 3)), dma, dma, dma,
        ],
        compiler_params=pltpu.CompilerParams(collective_id=0, has_side_effects=True, vmem_limit_bytes=56 << 20),
        name="step",
    )(excite, present_inverse, retarded, columns, future_in)
    return pl.pallas_call(
        write_kernel,
        out_shape=results,
        in_specs=[vmem, vmem],
        out_specs=(hbm, hbm),
        scratch_shapes=[dma((2,))],
        compiler_params=pltpu.CompilerParams(vmem_limit_bytes=4 << 20),
        name="write",
    )(*held)


def solution(mesh):
    return jax.shard_map(
        per_device,
        mesh=mesh,
        in_specs=(
            P(None, "row", None),
            P("row", None, None),
            P("delay", "row", None, None, None),
            P("delay", "row", None),
            P("delay", "row", None),
        ),
        out_specs=(P(None, "row", None), P("delay", "row", None)),
        check_vma=False,
    )
```

```python
import jax
import jax.numpy as jnp
from jax import lax
from jax.experimental import pallas as pl
from jax.experimental.pallas import tpu as pltpu
from jax.sharding import PartitionSpec as P

MESH = pl.DeviceIdType.MESH
BLK = 128
ROWS = 512
RB = 4
NNZ = 16
WID = 128
HOPS = (1, 3, 2)
SENDS = (2, 1, 3)
ORDER = sorted(range(32), key=lambda p: -(min((p // 4) % 4, 4 - (p // 4) % 4) + min(p % 4, 4 - p % 4)))
REACH = 4


def step_kernel(
    excite, inverse, weights, columns, future, currents, out,
    ex_v, inv_v, w_v, col_s, fut_v, cast_v, shift_v, pass_v, half_v, src_v, row_v, whole,
    load_sem, pass_send, pass_recv, half_send, half_recv, one_send, one_recv, few_send, few_recv,
    line_send, line_recv, fwd_send, ready, ready_shift,
    all_send, direct_send, a_recv, b_recv, c_recv, sh_send, sh_recv,
):
    d = lax.axis_index("delay")
    r = lax.axis_index("row")
    core = d % 2
    zh = (d // 2) % 2
    x = (d // 4) % 4
    y = d // 16
    z = zh * 8 + r
    step_a = 4 + 12 * core
    step_b = 16 - 12 * core
    a = x * (1 - core) + y * core
    b = y * (1 - core) + x * core
    base = d - zh * 2
    mine = core * 16 + b * 4 + a
    near = zh == 0
    far = zh == 1
    root = (x + y + zh) == 0
    source = d == 0
    partner = (d + 1 - 2 * core, r)

    def rank_of(line):
        return jnp.where(line < 8, line, 23 - line)

    rank = rank_of(z)

    def wrapped(k):
        return (z + k + 16) % 16

    def at_z(k):
        n = wrapped(k)
        return (base + (n // 8) * 2, n % 8)

    def later(k):
        return rank_of(wrapped(k)) > rank

    def peer_a(k):
        return (d + ((a + k) % 4 - a) * step_a, r)

    def peer_b(k):
        return (d + ((b + k) % 4 - b) * step_b, r)

    def remote(src, dst, send, recv, device):
        return pltpu.make_async_remote_copy(src, dst, send, recv, device_id=device, device_id_type=MESH)

    barrier = pltpu.get_barrier_semaphore()

    def greet(device):
        pl.semaphore_signal(barrier, inc=1, device_id=device, device_id_type=MESH)

    fut_in = pltpu.make_async_copy(future.at[0], fut_v, load_sem.at[0])
    fut_in.start()

    for k in HOPS:
        greet(peer_a(k))
        greet(peer_b(k))
    greet(partner)
    greeted = 7
    steps = [s * k for k in range(1, REACH + 1) for s in (1, -1)]
    for k in steps:
        @pl.when(later(k))
        def _(k=k):
            greet(at_z(k))
        greeted = greeted + jnp.where(later(k), 0, 1)
    for k in (5, 6):
        @pl.when((z + k < 8) & (z >= k - 5))
        def _(k=k):
            greet(at_z(k))
        greeted = greeted + jnp.where(near & (z >= k + k % 5), 1, 0)
    @pl.when(z == 0)
    def _():
        greet((0, 7))
        greet((0, 6))
    greeted = greeted + jnp.where(source & (r >= 6), 32, 0)

    @pl.when((d % 4 == 1))
    def _():
        greet((d + 2, r))

    @pl.when((d % 4 == 0) & (d > 0))
    def _():
        greet((d - 1, r))

    greeted = greeted + jnp.where(d % 4 == 3, 1, 0) + jnp.where((d % 4 == 3) & (d < 63), 1, 0)

    w_in = pltpu.make_async_copy(weights.at[0], w_v, load_sem.at[3])
    col_in = pltpu.make_async_copy(columns.at[0], col_s, load_sem.at[4])
    ex_in = pltpu.make_async_copy(excite.at[0], ex_v, load_sem.at[1])
    inv_in = pltpu.make_async_copy(inverse, inv_v, load_sem.at[2])

    @pl.when(source)
    def _():
        ex_in.start()
        inv_in.start()
        fut_in.wait()
        ex_in.wait()
        inv_in.wait()
        right = (ex_v[...].astype(jnp.float32) - fut_v[...]).astype(jnp.bfloat16)
        for k in range(RB):
            got = jnp.dot(inv_v[k], right[k * BLK:(k + 1) * BLK], preferred_element_type=jnp.float32)
            cut = got.astype(jnp.bfloat16).reshape(8, 16, WID)
            if k < 2:
                src_v[pl.ds(k * 8, 8)] = cut
            else:
                half_v[pl.ds(k * 8 - 16, 8)] = cut
            if k == 0:
                whole[0, r] = cut[0]

    w_in.start()
    col_in.start()

    @pl.when(d > 0)
    def _():
        fut_in.wait()
        cast_v[...] = fut_v[...].astype(jnp.bfloat16)

    pl.semaphore_wait(barrier, greeted)

    for k in steps:
        n = wrapped(k)
        sends = (n < 8) | ((n >= 12) & far & (n - z <= 3))
        @pl.when(jnp.logical_not(later(k)) & sends)
        def _(k=k):
            pl.semaphore_signal(ready.at[REACH - k], inc=1, device_id=at_z(k), device_id_type=MESH)

    @pl.when((d % 4 == 3) & (d < 63))
    def _():
        pl.semaphore_signal(ready_shift, inc=1, device_id=(d + 1, r), device_id_type=MESH)

    half_one = remote(half_v.at[0], whole.at[16, r], half_send, one_recv, partner)
    half_rest = remote(half_v.at[pl.ds(1, 15)], src_v.at[pl.ds(1, 15)], half_send, half_recv, partner)

    @pl.when(source)
    def _():
        half_rest.start()
        half_one.start()

    def root_one(k):
        return remote(src_v.at[k * 4], whole.at[core * 16 + k * 4, r], one_send, one_recv, peer_b(k))

    def root_few(k):
        return remote(
            src_v.at[pl.ds(k * 4 + 1, 3)], row_v.at[pl.ds(1, 3)], few_send, few_recv, peer_b(k)
        )

    def root_own(k):
        return remote(src_v.at[k], whole.at[core * 16 + k, r], one_send, one_recv, peer_a(k))

    def row_one(k):
        return remote(row_v.at[k], whole.at[core * 16 + b * 4 + k, r], one_send, one_recv, peer_a(k))

    @pl.when(root & (core == 1))
    def _():
        half_rest.wait_recv()

    @pl.when(root)
    def _():
        for k in (2, 1, 3):
            root_few(k).start()
        for k in (2, 1, 3):
            root_one(k).start()
            root_own(k).start()

    @pl.when(source & (r >= 6))
    def _():
        for p in ORDER:
            pc, pb, pa = p // 16, (p // 4) % 4, p % 4
            px, py = (pb, pa) if pc else (pa, pb)
            remote(
                half_v.at[p - 16] if pc else src_v.at[p], whole.at[p, r], direct_send, line_recv.at[r],
                ((py * 4 + px) * 4 + pc, 0),
            ).start()

    head = near & (a == 0) & (b > 0)

    @pl.when(head)
    def _():
        root_few(1).wait_recv()
        for k in (2, 1, 3):
            row_one(k).start()

    shift_copy = remote(cast_v, shift_v, sh_send, sh_recv, (d - 1, r))

    handed = remote(cast_v, pass_v, pass_send, pass_recv, partner)
    passed_on = remote(pass_v, shift_v, pass_send, sh_recv, (d - 2, r))

    @pl.when(core == 1)
    def _():
        shift_copy.start()

    @pl.when(far & (core == 0))
    def _():
        handed.start()

    @pl.when(near & (d > 0))
    def _():
        root_own(1).wait_recv()

    def line_copy(k):
        return remote(whole.at[mine, r], whole.at[mine, r], line_send, line_recv.at[r], at_z(k))

    @pl.when(near)
    def _():
        for k in (6, 5, 4, 3, 2, 1):
            @pl.when(z >= k + k // 6)
            def _(k=k):
                line_copy(-k).start()
        for k in (1, 2, 3, 4):
            pl.semaphore_wait(ready.at[REACH + k], 1)
            line_copy(k).start()
        for k in (1, 2, 3, 4):
            @pl.when(later(-k))
            def _(k=k):
                pl.semaphore_wait(ready.at[REACH - k], 1)
                line_copy(-k).start()

    def fwd_copy(k):
        s = z - 4 if k > 0 else (z + 4) % 16
        return remote(
            whole.at[mine, s], whole.at[mine, s], fwd_send, line_recv.at[s], at_z(k)
        )

    def got_piece(s):
        remote(whole.at[mine, s], whole.at[mine, s], half_send, line_recv.at[s], partner).wait_recv()

    def slab(k):
        return core * 16 + b * 4 + (a + 4 - k) % 4

    def part(p, g):
        return whole.at[p, pl.ds(g * 4, 4)]

    def lane(m, g):
        return whole.at[pl.ds(core * 16 + ((b + 4 - m) % 4) * 4, 4), pl.ds(g * 4, 4)]

    def copy_a(g, k):
        here = part(mine, g)
        return remote(here, here, all_send, a_recv.at[g, k - 1], peer_a(k))

    def copy_b(g, k, m):
        here = part(slab(k), g)
        return remote(here, here, all_send, b_recv.at[g, m - 1], peer_b(m))

    def copy_c(g, m):
        here = lane(m, g)
        return remote(here, here, all_send, c_recv, partner)

    plus = [((z >= 4) & (z < 8)), ((z >= 8) & (z < 12))]
    minus = [(z >= 12), (z < 4)]
    def forward_up(h):
        @pl.when(plus[h])
        def _():
            got_piece(z - 4)
            for k in (4, 3, 2, 1):
                fwd_copy(k).start()

    def forward_down(h):
        @pl.when(minus[h])
        def _():
            got_piece((z + 4) % 16)
            for k in (-3, -2, -1):
                if h == 0:
                    pl.semaphore_wait(ready.at[REACH + k], 1)
                    fwd_copy(k).start()
                else:
                    @pl.when(z + k < 0)
                    def _(k=k):
                        fwd_copy(k).start()

    def pieces(g):
        for s in range(g * 4, g * 4 + 4):
            passed = (plus[g] & (z - 4 == s)) | (minus[g] & ((z + 4) % 16 == s))

            @pl.when((far | (r != s)) & jnp.logical_not(passed))
            def _(s=s):
                got_piece(s)

    def spread(g):
        for k in SENDS:
            copy_a(g, k).start()
        for m in SENDS:
            copy_b(g, 0, m).start()

    def pass_on(g):
        for k in HOPS:
            copy_a(g, k).wait_recv()
            for m in SENDS:
                copy_b(g, k, m).start()
        copy_c(g, 0).start()

    def share(g):
        for m in HOPS:
            here = lane(m, g)
            remote(here, here, all_send, b_recv.at[g, m - 1], partner).wait_recv()
            copy_c(g, m).start()

    forward_up(0)
    forward_down(0)
    forward_up(1)

    @pl.when(far & (core == 1))
    def _():
        handed.wait_recv()
        passed_on.start()

    pieces(0)
    spread(0)
    forward_down(1)
    pass_on(0)
    pieces(1)
    spread(1)

    @pl.when((core == 0) & near & (d > 0))
    def _():
        pl.semaphore_wait(ready_shift, 1)
        shift_copy.start()


    share(0)
    pass_on(1)

    share(1)

    def drained(src, sem):
        remote(src, src, sem, c_recv, partner).wait_send()

    @pl.when(source)
    def _():
        drained(src_v, half_send)

    @pl.when(source & (r >= 6))
    def _():
        drained(whole.at[pl.ds(0, 4)], direct_send)

    @pl.when(root)
    def _():
        drained(src_v.at[pl.ds(0, 9)], few_send)
        drained(src_v.at[pl.ds(0, 6)], one_send)

    @pl.when(head)
    def _():
        drained(src_v.at[pl.ds(0, 3)], one_send)

    for low, high, count in ((0, 4, 8), (5, 6, 9), (7, 7, 10)):
        @pl.when((z >= low) & (z <= high))
        def _(count=count):
            drained(src_v.at[pl.ds(0, count)], line_send)

    for low, high, count in ((0, 0, 3), (1, 1, 2), (2, 2, 1), (4, 11, 4), (12, 15, 3)):
        @pl.when((z >= low) & (z <= high))
        def _(count=count):
            drained(src_v.at[pl.ds(0, count)], fwd_send)

    w_in.wait()
    col_in.wait()
    there = whole.at[pl.ds(0, 16)]
    remote(there, there, all_send, c_recv, partner).wait_recv()

    @pl.when(d < 63)
    def _():
        shift_copy.wait_recv()

    @pl.when(d == 63)
    def _():
        shift_v[...] = jnp.zeros_like(shift_v)

    currents[0] = whole[:, r].reshape(ROWS, WID)
    for i in range(RB):
        left = jnp.concatenate([w_v[i, k] for k in range(NNZ)], axis=1)
        picked = []
        for k in range(NNZ):
            j = col_s[i, k]
            picked.append(whole[pl.ds((j % 4) * 8, 8), j // 4].reshape(BLK, WID))
        total = jnp.dot(left, jnp.concatenate(picked, axis=0), preferred_element_type=jnp.float32)
        rows = pl.ds(i * BLK, BLK)
        out[0, rows] = total + shift_v[rows].astype(jnp.float32)

    drained(whole.at[pl.ds(0, 31)], all_send)

    @pl.when((d > 0) & (near | (core == 1)))
    def _():
        shift_copy.wait_send()

    @pl.when(far & (core == 0))
    def _():
        handed.wait_send()

    @pl.when(far & (core == 1))
    def _():
        passed_on.wait_send()


def write_kernel(currents, out, currents_out, out_out, sem):
    first = pltpu.make_async_copy(out, out_out, sem.at[0])
    second = pltpu.make_async_copy(currents, currents_out, sem.at[1])
    first.start()
    second.start()
    first.wait()
    second.wait()


def per_device(excite, present_inverse, retarded, columns, future_in):
    hbm = pl.BlockSpec(memory_space=pl.ANY)
    vmem = pl.BlockSpec(memory_space=pltpu.VMEM)
    dma = pltpu.SemaphoreType.DMA
    flag = pltpu.SemaphoreType.REGULAR
    half, single = jnp.bfloat16, jnp.float32
    results = (
        jax.ShapeDtypeStruct((1, ROWS, WID), half),
        jax.ShapeDtypeStruct((1, ROWS, WID), single),
    )
    held = pl.pallas_call(
        step_kernel,
        out_shape=(pltpu.VMEM((1, ROWS, WID), half), pltpu.VMEM((1, ROWS, WID), single)),
        in_specs=[hbm] * 5,
        out_specs=(vmem, vmem),
        scratch_shapes=[
            pltpu.VMEM((ROWS, WID), half),
            pltpu.VMEM((RB, BLK, BLK), half),
            pltpu.VMEM((RB, NNZ, BLK, BLK), half),
            pltpu.SMEM((RB, NNZ), jnp.int32),
            pltpu.VMEM((ROWS, WID), single),
            pltpu.VMEM((ROWS, WID), half),
            pltpu.VMEM((ROWS, WID), half),
            pltpu.VMEM((ROWS, WID), half),
            pltpu.VMEM((16, 16, WID), half),
            pltpu.VMEM((16, 16, WID), half),
            pltpu.VMEM((4, 16, WID), half),
            pltpu.VMEM((32, 8, 16, WID), half),
            dma((5,)), dma, dma, dma, dma, dma, dma, dma, dma,
            dma, dma((8,)), dma, flag((9,)), flag,
            dma, dma, dma((2, 3)), dma((2, 3)), dma, dma, dma,
        ],
        compiler_params=pltpu.CompilerParams(collective_id=0, has_side_effects=True, vmem_limit_bytes=56 << 20),
        name="step",
    )(excite, present_inverse, retarded, columns, future_in)
    return pl.pallas_call(
        write_kernel,
        out_shape=results,
        in_specs=[vmem, vmem],
        out_specs=(hbm, hbm),
        scratch_shapes=[dma((2,))],
        compiler_params=pltpu.CompilerParams(vmem_limit_bytes=4 << 20),
        name="write",
    )(*held)


def solution(mesh):
    return jax.shard_map(
        per_device,
        mesh=mesh,
        in_specs=(
            P(None, "row", None),
            P("row", None, None),
            P("delay", "row", None, None, None),
            P("delay", "row", None),
            P("delay", "row", None),
        ),
        out_specs=(P(None, "row", None), P("delay", "row", None)),
        check_vma=False,
    )
```

```python
import jax
import jax.numpy as jnp
from jax import lax
from jax.experimental import pallas as pl
from jax.experimental.pallas import tpu as pltpu
from jax.sharding import PartitionSpec as P

MESH = pl.DeviceIdType.MESH
BLK = 128
ROWS = 512
RB = 4
NNZ = 16
WID = 128
HOPS = (1, 3, 2)
SENDS = (2, 1, 3)
ORDER = sorted(range(32), key=lambda p: -(min((p // 4) % 4, 4 - (p // 4) % 4) + min(p % 4, 4 - p % 4)))
REACH = 4


def step_kernel(
    excite, inverse, weights, columns, future, currents, out,
    ex_v, inv_v, w_v, col_s, fut_v, cast_v, shift_v, pass_v, half_v, src_v, row_v, whole,
    load_sem, pass_send, pass_recv, half_send, half_recv, one_send, one_recv, few_send, few_recv,
    line_send, line_recv, fwd_send, ready, ready_shift,
    all_send, direct_send, a_recv, b_recv, c_recv, sh_send, sh_recv,
):
    d = lax.axis_index("delay")
    r = lax.axis_index("row")
    core = d % 2
    zh = (d // 2) % 2
    x = (d // 4) % 4
    y = d // 16
    z = zh * 8 + r
    step_a = 4 + 12 * core
    step_b = 16 - 12 * core
    a = x * (1 - core) + y * core
    b = y * (1 - core) + x * core
    base = d - zh * 2
    mine = core * 16 + b * 4 + a
    near = zh == 0
    far = zh == 1
    root = (x + y + zh) == 0
    source = d == 0
    partner = (d + 1 - 2 * core, r)

    def rank_of(line):
        return jnp.where(line < 8, line, 23 - line)

    rank = rank_of(z)

    def wrapped(k):
        return (z + k + 16) % 16

    def at_z(k):
        n = wrapped(k)
        return (base + (n // 8) * 2, n % 8)

    def later(k):
        return rank_of(wrapped(k)) > rank

    def peer_a(k):
        return (d + ((a + k) % 4 - a) * step_a, r)

    def peer_b(k):
        return (d + ((b + k) % 4 - b) * step_b, r)

    def remote(src, dst, send, recv, device):
        return pltpu.make_async_remote_copy(src, dst, send, recv, device_id=device, device_id_type=MESH)

    barrier = pltpu.get_barrier_semaphore()

    def greet(device):
        pl.semaphore_signal(barrier, inc=1, device_id=device, device_id_type=MESH)

    fut_in = pltpu.make_async_copy(future.at[0], fut_v, load_sem.at[0])
    fut_in.start()

    for k in HOPS:
        greet(peer_a(k))
        greet(peer_b(k))
    greet(partner)
    greeted = 7
    steps = [s * k for k in range(1, REACH + 1) for s in (1, -1)]
    for k in steps:
        @pl.when(later(k))
        def _(k=k):
            greet(at_z(k))
        greeted = greeted + jnp.where(later(k), 0, 1)
    for k in (5, 6):
        @pl.when((z + k < 8) & (z > 0))
        def _(k=k):
            greet(at_z(k))
        greeted = greeted + jnp.where(near & (z > k), 1, 0)
    @pl.when(z == 0)
    def _():
        for k in range(1, 8):
            greet((0, k))
    greeted = greeted + jnp.where(source & (r > 0), 32, 0)

    @pl.when((d % 4 == 1))
    def _():
        greet((d + 2, r))

    @pl.when((d % 4 == 0) & (d > 0))
    def _():
        greet((d - 1, r))

    greeted = greeted + jnp.where(d % 4 == 3, 1, 0) + jnp.where((d % 4 == 3) & (d < 63), 1, 0)

    w_in = pltpu.make_async_copy(weights.at[0], w_v, load_sem.at[3])
    col_in = pltpu.make_async_copy(columns.at[0], col_s, load_sem.at[4])
    ex_in = pltpu.make_async_copy(excite.at[0], ex_v, load_sem.at[1])
    inv_in = pltpu.make_async_copy(inverse, inv_v, load_sem.at[2])

    @pl.when(source)
    def _():
        ex_in.start()
        inv_in.start()
        fut_in.wait()
        ex_in.wait()
        inv_in.wait()
        right = (ex_v[...].astype(jnp.float32) - fut_v[...]).astype(jnp.bfloat16)
        for k in range(RB):
            got = jnp.dot(inv_v[k], right[k * BLK:(k + 1) * BLK], preferred_element_type=jnp.float32)
            cut = got.astype(jnp.bfloat16).reshape(8, 16, WID)
            if k < 2:
                src_v[pl.ds(k * 8, 8)] = cut
            else:
                half_v[pl.ds(k * 8 - 16, 8)] = cut
            if k == 0:
                whole[0, r] = cut[0]

    w_in.start()
    col_in.start()

    @pl.when(d > 0)
    def _():
        fut_in.wait()
        cast_v[...] = fut_v[...].astype(jnp.bfloat16)

    pl.semaphore_wait(barrier, greeted)

    for k in steps:
        n = wrapped(k)
        sends = (n < 8) | ((n >= 12) & far & (n - z <= 3))
        @pl.when(jnp.logical_not(later(k)) & sends)
        def _(k=k):
            pl.semaphore_signal(ready.at[REACH - k], inc=1, device_id=at_z(k), device_id_type=MESH)

    @pl.when((d % 4 == 3) & (d < 63))
    def _():
        pl.semaphore_signal(ready_shift, inc=1, device_id=(d + 1, r), device_id_type=MESH)

    half_one = remote(half_v.at[0], whole.at[16, r], half_send, one_recv, partner)
    half_rest = remote(half_v.at[pl.ds(1, 15)], src_v.at[pl.ds(1, 15)], half_send, half_recv, partner)

    @pl.when(source)
    def _():
        half_rest.start()
        half_one.start()

    def root_one(k):
        return remote(src_v.at[k * 4], whole.at[core * 16 + k * 4, r], one_send, one_recv, peer_b(k))

    def root_few(k):
        return remote(
            src_v.at[pl.ds(k * 4 + 1, 3)], row_v.at[pl.ds(1, 3)], few_send, few_recv, peer_b(k)
        )

    def root_own(k):
        return remote(src_v.at[k], whole.at[core * 16 + k, r], one_send, one_recv, peer_a(k))

    def row_one(k):
        return remote(row_v.at[k], whole.at[core * 16 + b * 4 + k, r], one_send, one_recv, peer_a(k))

    @pl.when(root & (core == 1))
    def _():
        half_rest.wait_recv()

    @pl.when(root)
    def _():
        for k in (2, 1, 3):
            root_few(k).start()
        for k in (2, 1, 3):
            root_one(k).start()
            root_own(k).start()

    @pl.when(source & (r > 0))
    def _():
        for p in ORDER:
            pc, pb, pa = p // 16, (p // 4) % 4, p % 4
            px, py = (pb, pa) if pc else (pa, pb)
            remote(
                half_v.at[p - 16] if pc else src_v.at[p], whole.at[p, r], direct_send, line_recv.at[r],
                ((py * 4 + px) * 4 + pc, 0),
            ).start()

    head = near & (a == 0) & (b > 0)

    @pl.when(head)
    def _():
        root_few(1).wait_recv()
        for k in (2, 1, 3):
            row_one(k).start()

    shift_copy = remote(cast_v, shift_v, sh_send, sh_recv, (d - 1, r))

    handed = remote(cast_v, pass_v, pass_send, pass_recv, partner)
    passed_on = remote(pass_v, shift_v, pass_send, sh_recv, (d - 2, r))

    @pl.when(core == 1)
    def _():
        shift_copy.start()

    @pl.when(far & (core == 0))
    def _():
        handed.start()

    @pl.when(near & (d > 0))
    def _():
        root_own(1).wait_recv()

    def line_copy(k):
        return remote(whole.at[mine, r], whole.at[mine, r], line_send, line_recv.at[r], at_z(k))

    @pl.when(near)
    def _():
        for k in (6, 5, 4, 3, 2, 1):
            @pl.when(z > k)
            def _(k=k):
                line_copy(-k).start()
        for k in (1, 2, 3, 4):
            pl.semaphore_wait(ready.at[REACH + k], 1)
            line_copy(k).start()
        for k in (1, 2, 3, 4):
            @pl.when(later(-k) & (z > 0))
            def _(k=k):
                pl.semaphore_wait(ready.at[REACH - k], 1)
                line_copy(-k).start()

    def fwd_copy(k):
        s = z - 4 if k > 0 else (z + 4) % 16
        return remote(
            whole.at[mine, s], whole.at[mine, s], fwd_send, line_recv.at[s], at_z(k)
        )

    def got_piece(s):
        remote(whole.at[mine, s], whole.at[mine, s], half_send, line_recv.at[s], partner).wait_recv()

    def slab(k):
        return core * 16 + b * 4 + (a + 4 - k) % 4

    def part(p, g):
        return whole.at[p, pl.ds(g * 4, 4)]

    def lane(m, g):
        return whole.at[pl.ds(core * 16 + ((b + 4 - m) % 4) * 4, 4), pl.ds(g * 4, 4)]

    def copy_a(g, k):
        here = part(mine, g)
        return remote(here, here, all_send, a_recv.at[g, k - 1], peer_a(k))

    def copy_b(g, k, m):
        here = part(slab(k), g)
        return remote(here, here, all_send, b_recv.at[g, m - 1], peer_b(m))

    def copy_c(g, m):
        here = lane(m, g)
        return remote(here, here, all_send, c_recv, partner)

    plus = [((z >= 4) & (z < 8)), ((z >= 8) & (z < 12))]
    minus = [(z >= 12), (z < 0), (z < 4)]
    def forward_up(h):
        @pl.when(plus[h])
        def _():
            got_piece(z - 4)
            for k in (4, 3, 2, 1):
                fwd_copy(k).start()

    def forward_down(h):
        @pl.when(minus[h])
        def _():
            got_piece((z + 4) % 16)
            for k in (-3, -2, -1):
                if h == 0:
                    pl.semaphore_wait(ready.at[REACH + k], 1)
                    fwd_copy(k).start()
                else:
                    @pl.when(z + k < 0)
                    def _(k=k):
                        fwd_copy(k).start()

    def pieces(g):
        for s in range(g * 4, g * 4 + 4):
            passed = (plus[g] & (z - 4 == s)) | ((minus[g] | minus[2]) & ((z + 4) % 16 == s))

            @pl.when((far | (r != s)) & jnp.logical_not(passed))
            def _(s=s):
                got_piece(s)

    def spread(g):
        for k in SENDS:
            copy_a(g, k).start()
        for m in SENDS:
            copy_b(g, 0, m).start()

    def pass_on(g):
        for k in HOPS:
            copy_a(g, k).wait_recv()
            for m in SENDS:
                copy_b(g, k, m).start()
        copy_c(g, 0).start()

    def share(g):
        for m in HOPS:
            here = lane(m, g)
            remote(here, here, all_send, b_recv.at[g, m - 1], partner).wait_recv()
            copy_c(g, m).start()

    forward_up(0)
    forward_down(0)
    forward_up(1)

    @pl.when(far & (core == 1))
    def _():
        handed.wait_recv()
        passed_on.start()

    pieces(0)
    spread(0)

    @pl.when(z == 0)
    def _():
        for k in (1, 2, 3, 4):
            pl.semaphore_wait(ready.at[REACH - k], 1)
            line_copy(-k).start()

    pass_on(0)
    forward_down(2)
    pieces(1)
    spread(1)

    @pl.when((core == 0) & near & (d > 0))
    def _():
        pl.semaphore_wait(ready_shift, 1)
        shift_copy.start()


    share(0)
    pass_on(1)

    share(1)

    def drained(src, sem):
        remote(src, src, sem, c_recv, partner).wait_send()

    @pl.when(source)
    def _():
        drained(src_v, half_send)

    @pl.when(source & (r > 0))
    def _():
        drained(whole.at[pl.ds(0, 4)], direct_send)

    @pl.when(root)
    def _():
        drained(src_v.at[pl.ds(0, 9)], few_send)
        drained(src_v.at[pl.ds(0, 6)], one_send)

    @pl.when(head)
    def _():
        drained(src_v.at[pl.ds(0, 3)], one_send)

    for low, high, count in ((0, 0, 8), (1, 4, 7), (5, 5, 8), (6, 6, 9), (7, 7, 10)):
        @pl.when((z >= low) & (z <= high))
        def _(count=count):
            drained(src_v.at[pl.ds(0, count)], line_send)

    for low, high, count in ((0, 0, 3), (1, 1, 2), (2, 2, 1), (4, 11, 4), (12, 15, 3)):
        @pl.when((z >= low) & (z <= high))
        def _(count=count):
            drained(src_v.at[pl.ds(0, count)], fwd_send)

    w_in.wait()
    col_in.wait()
    there = whole.at[pl.ds(0, 16)]
    remote(there, there, all_send, c_recv, partner).wait_recv()

    @pl.when(d < 63)
    def _():
        shift_copy.wait_recv()

    @pl.when(d == 63)
    def _():
        shift_v[...] = jnp.zeros_like(shift_v)

    currents[0] = whole[:, r].reshape(ROWS, WID)
    for i in range(RB):
        left = jnp.concatenate([w_v[i, k] for k in range(NNZ)], axis=1)
        picked = []
        for k in range(NNZ):
            j = col_s[i, k]
            picked.append(whole[pl.ds((j % 4) * 8, 8), j // 4].reshape(BLK, WID))
        total = jnp.dot(left, jnp.concatenate(picked, axis=0), preferred_element_type=jnp.float32)
        rows = pl.ds(i * BLK, BLK)
        out[0, rows] = total + shift_v[rows].astype(jnp.float32)

    drained(whole.at[pl.ds(0, 31)], all_send)

    @pl.when((d > 0) & (near | (core == 1)))
    def _():
        shift_copy.wait_send()

    @pl.when(far & (core == 0))
    def _():
        handed.wait_send()

    @pl.when(far & (core == 1))
    def _():
        passed_on.wait_send()


def write_kernel(currents, out, currents_out, out_out, sem):
    first = pltpu.make_async_copy(out, out_out, sem.at[0])
    second = pltpu.make_async_copy(currents, currents_out, sem.at[1])
    first.start()
    second.start()
    first.wait()
    second.wait()


def per_device(excite, present_inverse, retarded, columns, future_in):
    hbm = pl.BlockSpec(memory_space=pl.ANY)
    vmem = pl.BlockSpec(memory_space=pltpu.VMEM)
    dma = pltpu.SemaphoreType.DMA
    flag = pltpu.SemaphoreType.REGULAR
    half, single = jnp.bfloat16, jnp.float32
    results = (
        jax.ShapeDtypeStruct((1, ROWS, WID), half),
        jax.ShapeDtypeStruct((1, ROWS, WID), single),
    )
    held = pl.pallas_call(
        step_kernel,
        out_shape=(pltpu.VMEM((1, ROWS, WID), half), pltpu.VMEM((1, ROWS, WID), single)),
        in_specs=[hbm] * 5,
        out_specs=(vmem, vmem),
        scratch_shapes=[
            pltpu.VMEM((ROWS, WID), half),
            pltpu.VMEM((RB, BLK, BLK), half),
            pltpu.VMEM((RB, NNZ, BLK, BLK), half),
            pltpu.SMEM((RB, NNZ), jnp.int32),
            pltpu.VMEM((ROWS, WID), single),
            pltpu.VMEM((ROWS, WID), half),
            pltpu.VMEM((ROWS, WID), half),
            pltpu.VMEM((ROWS, WID), half),
            pltpu.VMEM((16, 16, WID), half),
            pltpu.VMEM((16, 16, WID), half),
            pltpu.VMEM((4, 16, WID), half),
            pltpu.VMEM((32, 8, 16, WID), half),
            dma((5,)), dma, dma, dma, dma, dma, dma, dma, dma,
            dma, dma((8,)), dma, flag((9,)), flag,
            dma, dma, dma((2, 3)), dma((2, 3)), dma, dma, dma,
        ],
        compiler_params=pltpu.CompilerParams(collective_id=0, has_side_effects=True, vmem_limit_bytes=56 << 20),
        name="step",
    )(excite, present_inverse, retarded, columns, future_in)
    return pl.pallas_call(
        write_kernel,
        out_shape=results,
        in_specs=[vmem, vmem],
        out_specs=(hbm, hbm),
        scratch_shapes=[dma((2,))],
        compiler_params=pltpu.CompilerParams(vmem_limit_bytes=4 << 20),
        name="write",
    )(*held)


def solution(mesh):
    return jax.shard_map(
        per_device,
        mesh=mesh,
        in_specs=(
            P(None, "row", None),
            P("row", None, None),
            P("delay", "row", None, None, None),
            P("delay", "row", None),
            P("delay", "row", None),
        ),
        out_specs=(P(None, "row", None), P("delay", "row", None)),
        check_vma=False,
    )
```
